32 devices in a mesh: band: 16 (over z, y, x), mem: 2 (over core).
Axes of the slice: x: 2, y: 2, z: 4, core: 2. Of those that a mesh axis runs over, the one named last changes fastest.
Arguments:
- state: float32 [16384, 2048], P('band', 'mem'), may hold values from -10 to 10
- obs_anom: bfloat16 [4096, 2048], P('band', 'mem'), may hold values from -8 to 8
- innov: float32 [4096, 2048], P('band', 'mem'), may hold values from -12 to 12
- pattern: int32 [16, 4, 8, 4], P('band'), may hold values 0 or 1
- distance: int32 [16, 4, 8, 4], P('band'), may hold values from 0 to 7
- taper: float32 [8], replicated, may hold values from 0.2 to 1
- order: int32 [16, 4], P('band'), may hold values from 0 to 3, each once within a row
Outputs:
- analysis: float32 [16384, 2048], P('band', 'mem')
The draws below stay inside these ranges and needn't reach their ends.
Inputs may be any that keep to these rules, and one draw needn't show every extreme that they name: Each row of order lists 0 .. 3 once each.
All inputs are finite; a program needn't handle non-finite values. No bound on the sum of `pattern` on one device may be relied on, other than what follows from the above.
Results may differ from the reference program's by a relative error of at most 0.0028.
Values may be sent and summed in bfloat16 or wider, within the bound.
A program may use at most 64 MiB of HBM per device.

```python
import jax
import jax.numpy as jnp
from jax import lax

SB = 1024
OBS = 256
ARR = 4
DMAX = 8
RBLK = 8
OBLK = 4
BANDS = 16
MEMBERS = 2048
N_BAND = 16


def rough_values(seed_key, shape):
    return jax.random.normal(seed_key, shape, jnp.float32)


def latent_fields(key):
    latent_count = OBS // 4
    fields = rough_values(jax.random.fold_in(key, 7001), (BANDS, latent_count, MEMBERS))
    return fields


def band_rows(fields, seed_key, reach_bands, row_count, jitter_scale):
    latent_count = fields.shape[1]
    width = reach_bands * latent_count

    def one_band(band_index):
        picked = jnp.concatenate([lax.dynamic_index_in_dim(fields, (band_index - shift_by) % BANDS, 0, keepdims=False) for shift_by in range(reach_bands)], axis=0)
        band_key = jax.random.fold_in(seed_key, band_index)
        mixing = jax.random.normal(jax.random.fold_in(band_key, 1), (row_count, width), jnp.float32) / jnp.sqrt(jnp.float32(width))
        jitter = rough_values(jax.random.fold_in(band_key, 2), (row_count, fields.shape[2]))
        return jnp.dot(mixing, picked, precision=lax.Precision.HIGHEST) + jitter_scale * jitter
    return lax.map(one_band, jnp.arange(BANDS, dtype=jnp.int32))


def observed(key):
    fields = latent_fields(key)
    return band_rows(fields, jax.random.fold_in(key, 7200), 2, OBS, 0.4).reshape(BANDS * OBS, MEMBERS)


def draw_state(key, part):
    fields = latent_fields(key)
    values = band_rows(fields, jax.random.fold_in(key, 7100), 5, SB, 0.5).reshape(BANDS * SB, MEMBERS)
    return jnp.clip(values, -10.0, 10.0)


def draw_obs_anom(key, part):
    return jnp.clip(observed(key), -8.0, 8.0).astype(jnp.bfloat16)


def draw_innov(key, part):
    anomaly = observed(key)
    offset = rough_values(jax.random.fold_in(key, 7301), (BANDS * OBS, 1))
    perturb = rough_values(jax.random.fold_in(key, 7300), (BANDS * OBS, MEMBERS))
    return jnp.clip(offset - anomaly + perturb, -12.0, 12.0)


def set_ends(values, own_key, least, largest):
    shape = values.shape
    spot = [jax.random.randint(jax.random.fold_in(own_key, axis), (), 0, shape[axis]) for axis in range(len(shape))]
    values = values.at[tuple(spot)].set(least)
    longest = shape.index(max(shape))
    spot[longest] = (spot[longest] + 1) % shape[longest]
    return values.at[tuple(spot)].set(largest)


def setup_inputs(seed: int = 0) -> dict:
    arg_keys = jax.random.split(jax.random.key(seed), 8)
    state = draw_state(jax.random.fold_in(arg_keys[7], 71), 0)
    obs_anom = draw_obs_anom(jax.random.fold_in(arg_keys[7], 71), 0)
    innov = draw_innov(jax.random.fold_in(arg_keys[7], 71), 0)
    pattern = set_ends((jax.random.randint(arg_keys[3], (BANDS, ARR, RBLK, OBLK), 0, 4) < 3).astype(jnp.int32), jax.random.fold_in(arg_keys[3], 1), 0, 1)
    distance = set_ends(jax.random.randint(arg_keys[4], (BANDS, ARR, RBLK, OBLK), 0, DMAX), jax.random.fold_in(arg_keys[4], 1), 0, DMAX - 1).astype(jnp.int32)
    taper = jnp.clip(jax.random.uniform(arg_keys[5], (DMAX,), jnp.float32, 0.2, 1.0), 0.2, 1.0)
    order = jax.vmap(lambda own: jax.random.permutation(own, ARR))(jax.random.split(arg_keys[6], BANDS)).reshape((BANDS, ARR)).astype(jnp.int32)
    return {"state": state, "obs_anom": obs_anom, "innov": innov, "pattern": pattern, "distance": distance, "taper": taper, "order": order}


def spread(blocks):
    rows, cols = blocks.shape
    return jnp.broadcast_to(blocks[:, None, :, None], (rows, 128, cols, 64)).reshape(rows * 128, cols * 64)

def reference(state, obs_anom, innov, pattern, distance, taper, order):
    members = state.shape[1]
    scale = 1.0 / (members - 1)
    y_three = obs_anom.reshape(N_BAND, OBS, members)
    d_three = innov.reshape(N_BAND, OBS, members)

    def weigh(pair):
        y_batch, d_batch = pair
        gram = jnp.dot(y_batch.astype(jnp.float32), y_batch.T.astype(jnp.float32), preferred_element_type=jnp.float32)
        spd = gram * scale + jnp.eye(OBS, dtype=jnp.float32)
        factor = jnp.linalg.cholesky(spd)
        return jax.scipy.linalg.cho_solve((factor, True), d_batch).astype(jnp.bfloat16)
    w_three = lax.map(weigh, (y_three, d_three))
    onehot = (distance[..., None] == jnp.arange(DMAX, dtype=jnp.int32)).astype(jnp.float32)
    local = pattern.astype(jnp.float32) * jnp.sum(onehot * taper, axis=-1)
    x_three = state.reshape(N_BAND, SB, members)

    def band_update(index):
        field = lax.dynamic_index_in_dim(x_three, index, 0, keepdims=False)
        for step in range(ARR):
            offset = order[index, step]
            source = (index - offset) % N_BAND
            y_batch = y_three[source].astype(jnp.float32)
            w_batch = w_three[source].astype(jnp.float32)
            weights = spread(local[index, offset])
            cross = jnp.dot(field, y_batch.T, precision=lax.Precision.HIGHEST)
            field = field + jnp.dot(cross * scale * weights, w_batch, precision=lax.Precision.HIGHEST)
        return field
    result = lax.map(band_update, jnp.arange(N_BAND, dtype=jnp.int32))
    return result.reshape(state.shape)
```

```python
import functools

import jax
import jax.numpy as jnp
from jax import lax
from jax.experimental import pallas as pl
from jax.experimental.pallas import tpu as pltpu
from jax.sharding import PartitionSpec as P

F32 = jnp.float32
BF16 = jnp.bfloat16
VMEM_SPEC = pl.BlockSpec(memory_space=pltpu.VMEM)
SMEM_SPEC = pl.BlockSpec(memory_space=pltpu.SMEM)


def from_behind(value, axis, steps):
    count = lax.axis_size(axis)
    pairs = [(source, (source + steps) % count) for source in range(count)]
    return lax.ppermute(value, axis, pairs)


def member_parts(value):
    if lax.axis_size("mem") == 2:
        return [value, from_behind(value, "mem", 1)]
    return [lax.psum(value, "mem")]


def halves(value):
    high = value.astype(BF16)
    return high, (value - high.astype(F32)).astype(BF16)


def mm(a, b):
    return jnp.dot(a, b, preferred_element_type=F32)


def mm3(a, b):
    a_high, a_low = halves(a)
    b_high, b_low = halves(b)
    return mm(a_high, b_high) + (mm(a_high, b_low) + mm(a_low, b_high))


def mm_full(a, b):
    return jnp.dot(a, b, precision=lax.Precision.HIGHEST, preferred_element_type=F32)


def nt(a, b):
    return lax.dot_general(a, b, (((1,), (1,)), ((), ())), preferred_element_type=F32)


def weigh_kernel(scale, part_count, *refs):
    parts = refs[:part_count]
    d_ref, w_ref, inv = refs[part_count:]
    total = parts[0][...]
    for part in parts[1:]:
        total = total + part[...]
    size = total.shape[0]
    eye = (
        lax.broadcasted_iota(jnp.int32, (size, size), 0)
        == lax.broadcasted_iota(jnp.int32, (size, size), 1)
    ).astype(F32)
    spd = total * scale + eye
    square = mm3(spd, spd)
    bound2 = jnp.max(jnp.sum(jnp.abs(square), axis=1))
    row = jnp.max(jnp.sum(jnp.abs(spd), axis=1))
    top = jnp.minimum(row, jnp.sqrt(bound2 * 1.01)) * 1.001
    ratio = (top - 1.0) / (top + 1.0)
    alpha = 2.0 / (top + 1.0)
    gain = 2.0 / (2.0 - ratio * ratio)
    c0 = 2.0 * alpha * gain
    c1 = -alpha * alpha * gain
    ratio = ratio * ratio * 0.5 * gain
    inv[...] = c0 * eye + c1 * spd
    small = top < 40.0

    def run(product, active):
        def going(ratio):
            return jnp.logical_and(active, ratio > 2e-5)

        def step(ratio):
            now = inv[...]
            gain = 2.0 / (2.0 - ratio * ratio)
            inv[...] = gain * (2.0 * now - product(now, product(spd, now)))
            return ratio * ratio * 0.5 * gain

        lax.while_loop(going, step, ratio)

    run(mm3, small)
    run(mm_full, jnp.logical_not(small))

    @pl.when(small)
    def _():
        w_ref[...] = mm3(inv[...], d_ref[...]).astype(BF16)

    @pl.when(jnp.logical_not(small))
    def _():
        now = inv[...]
        first = mm_full(now, d_ref[...])
        left = d_ref[...] - mm_full(spd, first)
        w_ref[...] = (first + mm_full(now, left)).astype(BF16)


def link_kernel(count, order_ref, *refs):
    ys = refs[:count]
    ws = refs[count : 2 * count]
    g_ref, sorted_ref, y_sorted = refs[2 * count :]
    for step in range(count):
        for offset in range(count):

            @pl.when(order_ref[0, step] == offset)
            def _():
                y_sorted[step] = ys[offset][...]
                sorted_ref[step] = ws[offset][...]

    place = 0
    for step in range(1, count):
        for before in range(step):
            g_ref[place] = nt(sorted_ref[before], y_sorted[step])
            place += 1


def apply_kernel(scale, count, part_count, *refs):
    order_ref, pattern_ref, distance_ref, taper_ref = refs[:4]
    refs = refs[4:]
    crosses = [refs[part_count * a : part_count * (a + 1)] for a in range(count)]
    refs = refs[part_count * count :]
    links = refs[:part_count]
    w_ref, x_ref, out_ref, cross_now = refs[part_count:]
    block = pl.program_id(0)
    cols = cross_now.shape[1]
    q_count = pattern_ref.shape[3]
    lane = lax.broadcasted_iota(jnp.int32, (1, cols), 1)
    applied = []
    field = x_ref[...]
    place = 0
    for step in range(count):
        offset = order_ref[0, step]
        for a in range(count):

            @pl.when(offset == a)
            def _():
                total = crosses[a][0][...]
                for part in crosses[a][1:]:
                    total = total + part[...]
                cross_now[...] = total

        weight = jnp.zeros((1, cols), F32)
        for q in range(q_count):
            value = pattern_ref[0, offset, block, q].astype(F32) * taper_ref[
                distance_ref[0, offset, block, q]
            ]
            inside = (lane >= q * (cols // q_count)) & (lane < (q + 1) * (cols // q_count))
            weight = jnp.where(inside, value, weight)
        cross = cross_now[...]
        for before in range(step):
            link = links[0][place]
            for part in links[1:]:
                link = link + part[place]
            place += 1
            link_high, link_low = halves(link)
            high, low = applied[before]
            cross = cross + (mm(high, link_high) + (mm(high, link_low) + mm(low, link_high)))
        applied.append(halves(cross * scale * weight))
        high, low = applied[-1]
        field = field + (mm(high, w_ref[step]) + mm(low, w_ref[step]))
    out_ref[...] = field


def on_device(state, obs_anom, innov, pattern, distance, taper, order):
    cells, own_members = state.shape
    members = lax.axis_size("mem") * own_members
    scale = 1.0 / (members - 1)
    num_obs = obs_anom.shape[0]
    arrivals = order.shape[1]
    row_blocks = pattern.shape[2]
    rows = cells // row_blocks
    gram_parts = member_parts(nt(obs_anom, obs_anom))
    ys = [obs_anom] + [from_behind(obs_anom, "band", a) for a in range(1, arrivals)]
    weights = pl.pallas_call(
        functools.partial(weigh_kernel, scale, len(gram_parts)),
        out_shape=jax.ShapeDtypeStruct(innov.shape, BF16),
        in_specs=[VMEM_SPEC] * (len(gram_parts) + 1),
        out_specs=VMEM_SPEC,
        scratch_shapes=[pltpu.VMEM((num_obs, num_obs), F32)],
        cost_estimate=pl.CostEstimate(
            flops=60 * num_obs**3, bytes_accessed=8 * innov.size, transcendentals=0
        ),
    )(*gram_parts, innov)
    ws = [weights] + [from_behind(weights, "band", a) for a in range(1, arrivals)]
    state_high = state.astype(BF16)
    crosses = [member_parts(nt(state_high, y)) for y in ys]
    pairs = arrivals * (arrivals - 1) // 2
    link, w_sorted = pl.pallas_call(
        functools.partial(link_kernel, arrivals),
        out_shape=(
            jax.ShapeDtypeStruct((pairs, num_obs, num_obs), F32),
            jax.ShapeDtypeStruct((arrivals,) + obs_anom.shape, BF16),
        ),
        in_specs=[SMEM_SPEC] + [VMEM_SPEC] * (2 * arrivals),
        out_specs=(VMEM_SPEC, VMEM_SPEC),
        scratch_shapes=[pltpu.VMEM((arrivals,) + obs_anom.shape, BF16)],
    )(order, *ys, *ws)
    links = member_parts(link)
    part_count = len(links)
    row_spec = pl.BlockSpec((rows, num_obs), lambda i: (i, 0))
    field_spec = pl.BlockSpec((rows, own_members), lambda i: (i, 0))
    return pl.pallas_call(
        functools.partial(apply_kernel, scale, arrivals, part_count),
        out_shape=jax.ShapeDtypeStruct(state.shape, F32),
        grid=(row_blocks,),
        in_specs=[SMEM_SPEC] * 4
        + [row_spec] * (arrivals * part_count)
        + [pl.BlockSpec((pairs, num_obs, num_obs), lambda i: (0, 0, 0))] * part_count
        + [pl.BlockSpec((arrivals,) + obs_anom.shape, lambda i: (0, 0, 0)), field_spec],
        out_specs=field_spec,
        scratch_shapes=[pltpu.VMEM((rows, num_obs), F32)],
    )(
        order,
        pattern,
        distance,
        taper,
        *[part for cross in crosses for part in cross],
        *links,
        w_sorted,
        state,
    )


def solution(mesh):
    return jax.shard_map(
        on_device,
        mesh=mesh,
        in_specs=(
            P("band", "mem"),
            P("band", "mem"),
            P("band", "mem"),
            P("band", None, None, None),
            P("band", None, None, None),
            P(),
            P("band", None),
        ),
        out_specs=P("band", "mem"),
        check_vma=False,
    )
```

```python
import functools

import jax
import jax.numpy as jnp
from jax import lax
from jax.experimental import pallas as pl
from jax.experimental.pallas import tpu as pltpu
from jax.sharding import PartitionSpec as P

F32 = jnp.float32
BF16 = jnp.bfloat16
VMEM_SPEC = pl.BlockSpec(memory_space=pltpu.VMEM)
SMEM_SPEC = pl.BlockSpec(memory_space=pltpu.SMEM)


def from_behind(value, axis, steps):
    count = lax.axis_size(axis)
    pairs = [(source, (source + steps) % count) for source in range(count)]
    return lax.ppermute(value, axis, pairs)


def member_parts(value):
    if lax.axis_size("mem") == 2:
        return [value, from_behind(value, "mem", 1)]
    return [lax.psum(value, "mem")]


def halves(value):
    high = value.astype(BF16)
    return high, (value - high.astype(F32)).astype(BF16)


def mm(a, b):
    return jnp.dot(a, b, preferred_element_type=F32)


def mm3(a, b):
    a_high, a_low = halves(a)
    b_high, b_low = halves(b)
    return mm(a_high, b_high) + (mm(a_high, b_low) + mm(a_low, b_high))


def mm_full(a, b):
    return jnp.dot(a, b, precision=lax.Precision.HIGHEST, preferred_element_type=F32)


def nt(a, b):
    return lax.dot_general(a, b, (((1,), (1,)), ((), ())), preferred_element_type=F32)


def weigh_kernel(scale, part_count, *refs):
    parts = refs[:part_count]
    d_ref, w_ref, inv = refs[part_count:]
    total = parts[0][...]
    for part in parts[1:]:
        total = total + part[...]
    size = total.shape[0]
    eye = (
        lax.broadcasted_iota(jnp.int32, (size, size), 0)
        == lax.broadcasted_iota(jnp.int32, (size, size), 1)
    ).astype(F32)
    spd = total * scale + eye
    square = mm3(spd, spd)
    bound2 = jnp.max(jnp.sum(jnp.abs(square), axis=1))
    row = jnp.max(jnp.sum(jnp.abs(spd), axis=1))
    top = jnp.minimum(row, jnp.sqrt(bound2 * 1.01)) * 1.001
    ratio = (top - 1.0) / (top + 1.0)
    alpha = 2.0 / (top + 1.0)
    gain = 2.0 / (2.0 - ratio * ratio)
    c0 = 2.0 * alpha * gain
    c1 = -alpha * alpha * gain
    ratio = ratio * ratio * 0.5 * gain
    inv[...] = c0 * eye + c1 * spd
    small = top < 40.0

    def run(product, active):
        def going(ratio):
            return jnp.logical_and(active, ratio > 2e-5)

        def step(ratio):
            now = inv[...]
            gain = 2.0 / (2.0 - ratio * ratio)
            inv[...] = gain * (2.0 * now - product(now, product(spd, now)))
            return ratio * ratio * 0.5 * gain

        lax.while_loop(going, step, ratio)

    run(mm3, small)
    run(mm_full, jnp.logical_not(small))

    @pl.when(small)
    def _():
        w_ref[...] = mm3(inv[...], d_ref[...]).astype(BF16)

    @pl.when(jnp.logical_not(small))
    def _():
        now = inv[...]
        first = mm_full(now, d_ref[...])
        left = d_ref[...] - mm_full(spd, first)
        w_ref[...] = (first + mm_full(now, left)).astype(BF16)


def grouped(group, bands):
    return bands % group == 0 and bands > group and group & (group - 1) == 0


def gathered(value, group):
    bands = lax.axis_size("band")
    if not grouped(group, bands):
        return [value] + [from_behind(value, "band", a) for a in range(1, group)]
    ahead = [(b, (b + group) % bands) for b in range(bands) if b % group]
    prior = lax.ppermute(value, "band", ahead)
    own_moves, prior_moves = [], []
    for flip in range(1, group):
        moves = [(b, b ^ flip) for b in range(bands)]
        up = [(b, to) for b, to in moves if to > b]
        down = [(b, to) for b, to in moves if to < b]
        own_moves.append(lax.ppermute(value, "band", up))
        prior_moves.append(lax.ppermute(prior, "band", down))
    return [value] + own_moves + prior_moves


def slots_of(order, group):
    offset = order[0]
    if not grouped(group, lax.axis_size("band")):
        return offset
    place = lax.axis_index("band") % group
    own = place ^ (place - offset)
    prior = group - 1 + (place ^ (place - offset + group))
    return jnp.where(offset == 0, 0, jnp.where(offset <= place, own, prior)).astype(jnp.int32)


def pick(slots_ref, arrays, target):
    for step in range(target.shape[0]):
        for slot, array in enumerate(arrays):

            @pl.when(slots_ref[step] == slot)
            def _():
                target[step] = array[...]


def cross_kernel(*refs):
    slots_ref, x_ref = refs[:2]
    arrays = refs[2:-2]
    cross_ref, y_ref = refs[-2:]

    @pl.when(pl.program_id(0) == 0)
    def _():
        pick(slots_ref, arrays, y_ref)

    high = x_ref[...].astype(BF16)
    for step in range(y_ref.shape[0]):
        cross_ref[step] = nt(high, y_ref[step])


def block_weight(tables, step, block, cols):
    order_ref, pattern_ref, distance_ref, taper_ref = tables
    q_count = pattern_ref.shape[3]
    width = cols // q_count
    lane = lax.broadcasted_iota(jnp.int32, (1, cols), 1)
    offset = order_ref[0, step]
    weight = jnp.zeros((1, cols), F32)
    for q in range(q_count):
        value = pattern_ref[0, offset, block, q].astype(F32) * taper_ref[
            distance_ref[0, offset, block, q]
        ]
        weight = jnp.where((lane >= q * width) & (lane < (q + 1) * width), value, weight)
    return weight


def prepare_kernel(scale, *refs):
    tables = refs[:4]
    parts = refs[4:-1]
    out_ref = refs[-1]
    count, _, cols = out_ref.shape
    for step in range(count):
        total = parts[0][step]
        for part in parts[1:]:
            total = total + part[step]
        weight = block_weight(tables, step, pl.program_id(0), cols)
        out_ref[step] = total * scale * weight


def link_kernel(*refs):
    slots_ref, y_ref = refs[:2]
    arrays = refs[2:-2]
    g_ref, w_ref = refs[-2:]
    pick(slots_ref, arrays, w_ref)
    place = 0
    for step in range(1, y_ref.shape[0]):
        for before in range(step):
            g_ref[place] = nt(w_ref[before], y_ref[step])
            place += 1


def apply_kernel(scale, per, *refs):
    tables = refs[:4]
    cross_ref = refs[4]
    links = refs[5:-5]
    w_ref, x_ref, out_ref, link_high, link_low = refs[-5:]
    count, rows, cols = cross_ref.shape

    @pl.when(pl.program_id(0) == 0)
    def _():
        total = links[0][...]
        for part in links[1:]:
            total = total + part[...]
        link_high[...], link_low[...] = halves(total)

    applied = []
    field = x_ref[...]
    place = 0
    for step in range(count):
        change = cross_ref[step]
        if step:
            more = jnp.zeros((rows, cols), F32)
            for high, low in applied:
                more = more + (
                    mm(high, link_high[place]) + (mm(high, link_low[place]) + mm(low, link_high[place]))
                )
                place += 1
            weight = jnp.concatenate(
                [
                    jnp.broadcast_to(
                        block_weight(tables, step, pl.program_id(0) * per + r, cols), (rows // per, cols)
                    )
                    for r in range(per)
                ],
                axis=0,
            )
            change = change + more * scale * weight
        applied.append(halves(change))
        high, low = applied[-1]
        field = field + (mm(high, w_ref[step]) + mm(low, w_ref[step]))
    out_ref[...] = field


def on_device(state, obs_anom, innov, pattern, distance, taper, order):
    cells, own_members = state.shape
    members = lax.axis_size("mem") * own_members
    scale = 1.0 / (members - 1)
    num_obs = obs_anom.shape[0]
    arrivals = order.shape[1]
    row_blocks = pattern.shape[2]
    rows = cells // row_blocks
    per = 2 if row_blocks % 2 == 0 else 1
    slots = slots_of(order, arrivals)
    gram_parts = member_parts(nt(obs_anom, obs_anom))
    ys = gathered(obs_anom, arrivals)
    weights = pl.pallas_call(
        functools.partial(weigh_kernel, scale, len(gram_parts)),
        out_shape=jax.ShapeDtypeStruct(innov.shape, BF16),
        in_specs=[VMEM_SPEC] * (len(gram_parts) + 1),
        out_specs=VMEM_SPEC,
        scratch_shapes=[pltpu.VMEM((num_obs, num_obs), F32)],
        cost_estimate=pl.CostEstimate(
            flops=60 * num_obs**3, bytes_accessed=8 * innov.size, transcendentals=0
        ),
    )(*gram_parts, innov)
    slots, weights = lax.optimization_barrier((slots, weights))
    ws = gathered(weights, arrivals)
    tall = per * rows
    row_spec = pl.BlockSpec((arrivals, tall, num_obs), lambda i: (0, i, 0))
    field_spec = pl.BlockSpec((tall, own_members), lambda i: (i, 0))
    batch_shape = (arrivals,) + obs_anom.shape
    batch_spec = pl.BlockSpec(batch_shape, lambda i: (0, 0, 0))
    cross_shape = jax.ShapeDtypeStruct((arrivals, cells, num_obs), F32)
    cross, y_sorted = pl.pallas_call(
        cross_kernel,
        out_shape=(cross_shape, jax.ShapeDtypeStruct(batch_shape, BF16)),
        grid=(row_blocks // per,),
        in_specs=[SMEM_SPEC, field_spec]
        + [pl.BlockSpec(obs_anom.shape, lambda i: (0, 0))] * len(ys),
        out_specs=(row_spec, batch_spec),
        cost_estimate=pl.CostEstimate(
            flops=2 * arrivals * state.size * num_obs, bytes_accessed=12 * state.size, transcendentals=0
        ),
    )(slots, state, *ys)
    crosses = member_parts(cross)
    tables = (order, pattern, distance, taper)
    prepared = pl.pallas_call(
        functools.partial(prepare_kernel, scale),
        out_shape=cross_shape,
        grid=(row_blocks,),
        in_specs=[SMEM_SPEC] * 4
        + [pl.BlockSpec((arrivals, rows, num_obs), lambda i: (0, i, 0))] * len(crosses),
        out_specs=pl.BlockSpec((arrivals, rows, num_obs), lambda i: (0, i, 0)),
    )(*tables, *crosses)
    ws, prepared = lax.optimization_barrier((ws, prepared))
    pairs = arrivals * (arrivals - 1) // 2
    link_shape = (pairs, num_obs, num_obs)
    link, w_sorted = pl.pallas_call(
        link_kernel,
        out_shape=(
            jax.ShapeDtypeStruct(link_shape, F32),
            jax.ShapeDtypeStruct(batch_shape, BF16),
        ),
        in_specs=[SMEM_SPEC] + [VMEM_SPEC] * (1 + len(ws)),
        out_specs=(VMEM_SPEC, VMEM_SPEC),
    )(slots, y_sorted, *ws)
    links = member_parts(link)
    return pl.pallas_call(
        functools.partial(apply_kernel, scale, per),
        out_shape=jax.ShapeDtypeStruct(state.shape, F32),
        grid=(row_blocks // per,),
        in_specs=[SMEM_SPEC] * 4
        + [row_spec]
        + [pl.BlockSpec(link_shape, lambda i: (0, 0, 0))] * len(links)
        + [batch_spec, field_spec],
        out_specs=field_spec,
        scratch_shapes=[pltpu.VMEM(link_shape, BF16), pltpu.VMEM(link_shape, BF16)],
    )(*tables, prepared, *links, w_sorted, state)


def solution(mesh):
    return jax.shard_map(
        on_device,
        mesh=mesh,
        in_specs=(
            P("band", "mem"),
            P("band", "mem"),
            P("band", "mem"),
            P("band", None, None, None),
            P("band", None, None, None),
            P(),
            P("band", None),
        ),
        out_specs=P("band", "mem"),
        check_vma=False,
    )
```

```python
import functools

import jax
import jax.numpy as jnp
from jax import lax
from jax.experimental import pallas as pl
from jax.experimental.pallas import tpu as pltpu
from jax.sharding import PartitionSpec as P


F32 = jnp.float32
BF16 = jnp.bfloat16
VMEM_SPEC = pl.BlockSpec(memory_space=pltpu.VMEM)
SMEM_SPEC = pl.BlockSpec(memory_space=pltpu.SMEM)


def from_behind(value, axis, steps):
    count = lax.axis_size(axis)
    pairs = [(source, (source + steps) % count) for source in range(count)]
    return lax.ppermute(value, axis, pairs)


def member_parts(value):
    if lax.axis_size("mem") == 2:
        return [value, from_behind(value, "mem", 1)]
    return [lax.psum(value, "mem")]


def halves(value):
    high = value.astype(BF16)
    return high, (value - high.astype(F32)).astype(BF16)


def mm(a, b):
    return jnp.dot(a, b, preferred_element_type=F32)


def mm3(a, b):
    a_high, a_low = halves(a)
    b_high, b_low = halves(b)
    return mm(a_high, b_high) + (mm(a_high, b_low) + mm(a_low, b_high))


def mm_full(a, b):
    return jnp.dot(a, b, precision=lax.Precision.HIGHEST, preferred_element_type=F32)


def nt(a, b):
    return lax.dot_general(a, b, (((1,), (1,)), ((), ())), preferred_element_type=F32)


def weigh_kernel(scale, part_count, *refs):
    parts = refs[:part_count]
    d_ref, w_ref, inv = refs[part_count:]
    total = parts[0][...]
    for part in parts[1:]:
        total = total + part[...]
    size = total.shape[0]
    eye = (
        lax.broadcasted_iota(jnp.int32, (size, size), 0)
        == lax.broadcasted_iota(jnp.int32, (size, size), 1)
    ).astype(F32)
    spd = total * scale + eye
    square = mm3(spd, spd)
    bound2 = jnp.max(jnp.sum(jnp.abs(square), axis=1))
    row = jnp.max(jnp.sum(jnp.abs(spd), axis=1))
    top = jnp.minimum(row, jnp.sqrt(bound2 * 1.01)) * 1.001
    ratio = (top - 1.0) / (top + 1.0)
    alpha = 2.0 / (top + 1.0)
    gain = 2.0 / (2.0 - ratio * ratio)
    c0 = 2.0 * alpha * gain
    c1 = -alpha * alpha * gain
    ratio = ratio * ratio * 0.5 * gain
    inv[...] = c0 * eye + c1 * spd
    small = top < 40.0

    def run(product, active):
        def going(ratio):
            return jnp.logical_and(active, ratio > 2e-5)

        def step(ratio):
            now = inv[...]
            gain = 2.0 / (2.0 - ratio * ratio)
            inv[...] = gain * (2.0 * now - product(now, product(spd, now)))
            return ratio * ratio * 0.5 * gain

        lax.while_loop(going, step, ratio)

    run(mm3, small)
    run(mm_full, jnp.logical_not(small))

    @pl.when(small)
    def _():
        w_ref[...] = mm3(inv[...], d_ref[...]).astype(BF16)

    @pl.when(jnp.logical_not(small))
    def _():
        now = inv[...]
        first = mm_full(now, d_ref[...])
        left = d_ref[...] - mm_full(spd, first)
        w_ref[...] = (first + mm_full(now, left)).astype(BF16)


def grouped(group, bands):
    return bands % group == 0 and bands > group and group & (group - 1) == 0


def gathered(value, group):
    bands = lax.axis_size("band")
    if not grouped(group, bands):
        return [value] + [from_behind(value, "band", a) for a in range(1, group)]
    prior = from_behind(value, "band", group)
    place = lax.axis_index("band") % group
    found = [value]
    for flip in range(1, group):
        upward = (place ^ flip) > place
        sent = jnp.where(upward, value, prior)
        found.append(lax.ppermute(sent, "band", [(b, b ^ flip) for b in range(bands)]))
    return found


def slots_of(order, group):
    offset = order[0]
    if not grouped(group, lax.axis_size("band")):
        return offset
    place = lax.axis_index("band") % group
    return (place ^ ((place - offset + group) % group)).astype(jnp.int32)


def pick(slots_ref, arrays, target):
    for step in range(target.shape[0]):
        for slot, array in enumerate(arrays):

            @pl.when(slots_ref[step] == slot)
            def _():
                target[step] = array[...]


def cross_kernel(*refs):
    slots_ref, x_ref = refs[:2]
    arrays = refs[2:-2]
    cross_ref, y_ref = refs[-2:]

    @pl.when(pl.program_id(0) == 0)
    def _():
        pick(slots_ref, arrays, y_ref)

    high = x_ref[...].astype(BF16)
    for step in range(y_ref.shape[0]):
        cross_ref[step] = nt(high, y_ref[step])


def block_weight(tables, step, block, cols):
    order_ref, pattern_ref, distance_ref, taper_ref = tables
    q_count = pattern_ref.shape[3]
    width = cols // q_count
    lane = lax.broadcasted_iota(jnp.int32, (1, cols), 1)
    offset = order_ref[0, step]
    weight = jnp.zeros((1, cols), F32)
    for q in range(q_count):
        value = pattern_ref[0, offset, block, q].astype(F32) * taper_ref[
            distance_ref[0, offset, block, q]
        ]
        weight = jnp.where((lane >= q * width) & (lane < (q + 1) * width), value, weight)
    return weight


def link_kernel(*refs):
    slots_ref, y_ref = refs[:2]
    arrays = refs[2:-2]
    g_ref, w_ref = refs[-2:]
    pick(slots_ref, arrays, w_ref)
    place = 0
    for step in range(1, y_ref.shape[0]):
        for before in range(step):
            g_ref[place] = nt(w_ref[before], y_ref[step])
            place += 1


def apply_kernel(scale, per, part_count, *refs):
    tables = refs[:4]
    crosses = refs[4 : 4 + part_count]
    links = refs[4 + part_count : -5]
    w_ref, x_ref, out_ref, link_high, link_low = refs[-5:]
    count, rows, cols = crosses[0].shape

    @pl.when(pl.program_id(0) == 0)
    def _():
        total = links[0][...]
        for part in links[1:]:
            total = total + part[...]
        link_high[...], link_low[...] = halves(total)

    applied = []
    field = x_ref[...]
    place = 0
    for step in range(count):
        total = crosses[0][step]
        for part in crosses[1:]:
            total = total + part[step]
        for high, low in applied:
            total = total + (
                mm(high, link_high[place]) + (mm(high, link_low[place]) + mm(low, link_high[place]))
            )
            place += 1
        weight = jnp.concatenate(
            [
                jnp.broadcast_to(
                    block_weight(tables, step, pl.program_id(0) * per + r, cols), (rows // per, cols)
                )
                for r in range(per)
            ],
            axis=0,
        )
        change = total * scale * weight
        applied.append(halves(change))
        high, low = applied[-1]
        field = field + (mm(high, w_ref[step]) + mm(low, w_ref[step]))
    out_ref[...] = field


def on_device(state, obs_anom, innov, pattern, distance, taper, order):
    cells, own_members = state.shape
    members = lax.axis_size("mem") * own_members
    scale = 1.0 / (members - 1)
    num_obs = obs_anom.shape[0]
    arrivals = order.shape[1]
    row_blocks = pattern.shape[2]
    rows = cells // row_blocks
    per = 2 if row_blocks % 2 == 0 else 1
    slots = slots_of(order, arrivals)
    gram_parts = member_parts(nt(obs_anom, obs_anom))
    ys = gathered(obs_anom, arrivals)
    solve = pl.pallas_call(
        functools.partial(weigh_kernel, scale, len(gram_parts)),
        out_shape=jax.ShapeDtypeStruct(innov.shape, BF16),
        in_specs=[VMEM_SPEC] * (len(gram_parts) + 1),
        out_specs=VMEM_SPEC,
        scratch_shapes=[pltpu.VMEM((num_obs, num_obs), F32)],
        cost_estimate=pl.CostEstimate(
            flops=60 * num_obs**3, bytes_accessed=8 * innov.size, transcendentals=0
        ),
    )
    weights = solve(*gram_parts, innov)
    slots, weights = lax.optimization_barrier((slots, weights))
    ws = gathered(weights, arrivals)
    tall = per * rows
    row_spec = pl.BlockSpec((arrivals, tall, num_obs), lambda i: (0, i, 0))
    field_spec = pl.BlockSpec((tall, own_members), lambda i: (i, 0))
    batch_shape = (arrivals,) + obs_anom.shape
    batch_spec = pl.BlockSpec(batch_shape, lambda i: (0, 0, 0))
    cross_shape = jax.ShapeDtypeStruct((arrivals, cells, num_obs), F32)
    cross_call = pl.pallas_call(
        cross_kernel,
        out_shape=(cross_shape, jax.ShapeDtypeStruct(batch_shape, BF16)),
        grid=(row_blocks // per,),
        in_specs=[SMEM_SPEC, field_spec]
        + [pl.BlockSpec(obs_anom.shape, lambda i: (0, 0))] * len(ys),
        out_specs=(row_spec, batch_spec),
        cost_estimate=pl.CostEstimate(
            flops=2 * arrivals * state.size * num_obs, bytes_accessed=12 * state.size, transcendentals=0
        ),
    )
    cross, y_sorted = cross_call(slots, state, *ys)
    crosses = member_parts(cross)
    tables = (order, pattern, distance, taper)
    ws, cross = lax.optimization_barrier((ws, crosses[0]))
    crosses = [cross] + crosses[1:]
    pairs = arrivals * (arrivals - 1) // 2
    link_shape = (pairs, num_obs, num_obs)
    link, w_sorted = pl.pallas_call(
        link_kernel,
        out_shape=(
            jax.ShapeDtypeStruct(link_shape, F32),
            jax.ShapeDtypeStruct(batch_shape, BF16),
        ),
        in_specs=[SMEM_SPEC] + [VMEM_SPEC] * (1 + len(ws)),
        out_specs=(VMEM_SPEC, VMEM_SPEC),
    )(slots, y_sorted, *ws)
    links = member_parts(link)
    return pl.pallas_call(
        functools.partial(apply_kernel, scale, per, len(crosses)),
        out_shape=jax.ShapeDtypeStruct(state.shape, F32),
        grid=(row_blocks // per,),
        in_specs=[SMEM_SPEC] * 4
        + [row_spec] * len(crosses)
        + [pl.BlockSpec(link_shape, lambda i: (0, 0, 0))] * len(links)
        + [batch_spec, field_spec],
        out_specs=field_spec,
        scratch_shapes=[pltpu.VMEM(link_shape, BF16), pltpu.VMEM(link_shape, BF16)],
    )(*tables, *crosses, *links, w_sorted, state)


def solution(mesh):
    return jax.shard_map(
        on_device,
        mesh=mesh,
        in_specs=(
            P("band", "mem"),
            P("band", "mem"),
            P("band", "mem"),
            P("band", None, None, None),
            P("band", None, None, None),
            P(),
            P("band", None),
        ),
        out_specs=P("band", "mem"),
        check_vma=False,
    )
```

```python
import functools

import jax
import jax.numpy as jnp
from jax import lax
from jax.experimental import pallas as pl
from jax.experimental.pallas import tpu as pltpu
from jax.sharding import PartitionSpec as P


F32 = jnp.float32
BF16 = jnp.bfloat16
VMEM_SPEC = pl.BlockSpec(memory_space=pltpu.VMEM)
SMEM_SPEC = pl.BlockSpec(memory_space=pltpu.SMEM)


def from_behind(value, axis, steps):
    count = lax.axis_size(axis)
    pairs = [(source, (source + steps) % count) for source in range(count)]
    return lax.ppermute(value, axis, pairs)


def member_parts(value):
    if lax.axis_size("mem") == 2:
        return [value, from_behind(value, "mem", 1)]
    return [lax.psum(value, "mem")]


def halves(value):
    high = value.astype(BF16)
    return high, (value - high.astype(F32)).astype(BF16)


def mm(a, b):
    return jnp.dot(a, b, preferred_element_type=F32)


def mm3(a, b):
    a_high, a_low = halves(a)
    b_high, b_low = halves(b)
    return mm(a_high, b_high) + (mm(a_high, b_low) + mm(a_low, b_high))


def mm_full(a, b):
    return jnp.dot(a, b, precision=lax.Precision.HIGHEST, preferred_element_type=F32)


def nt(a, b):
    return lax.dot_general(a, b, (((1,), (1,)), ((), ())), preferred_element_type=F32)


def weigh_kernel(scale, part_count, *refs):
    parts = refs[:part_count]
    d_ref, w_ref, inv = refs[part_count:]
    total = parts[0][...]
    for part in parts[1:]:
        total = total + part[...]
    size = total.shape[0]
    eye = (
        lax.broadcasted_iota(jnp.int32, (size, size), 0)
        == lax.broadcasted_iota(jnp.int32, (size, size), 1)
    ).astype(F32)
    spd = total * scale + eye
    square = mm3(spd, spd)
    bound2 = jnp.max(jnp.sum(jnp.abs(square), axis=1))
    row = jnp.max(jnp.sum(jnp.abs(spd), axis=1))
    top = jnp.minimum(row, jnp.sqrt(bound2 * 1.01)) * 1.001
    ratio = (top - 1.0) / (top + 1.0)
    alpha = 2.0 / (top + 1.0)
    gain = 2.0 / (2.0 - ratio * ratio)
    c0 = 2.0 * alpha * gain
    c1 = -alpha * alpha * gain
    ratio = ratio * ratio * 0.5 * gain
    inv[...] = c0 * eye + c1 * spd
    small = top < 40.0

    def run(product, active):
        def going(ratio):
            return jnp.logical_and(active, ratio > 2e-5)

        def step(ratio):
            now = inv[...]
            gain = 2.0 / (2.0 - ratio * ratio)
            inv[...] = gain * (2.0 * now - product(now, product(spd, now)))
            return ratio * ratio * 0.5 * gain

        lax.while_loop(going, step, ratio)

    run(mm3, small)
    run(mm_full, jnp.logical_not(small))

    @pl.when(small)
    def _():
        w_ref[...] = mm3(inv[...], d_ref[...]).astype(BF16)

    @pl.when(jnp.logical_not(small))
    def _():
        now = inv[...]
        first = mm_full(now, d_ref[...])
        left = d_ref[...] - mm_full(spd, first)
        w_ref[...] = (first + mm_full(now, left)).astype(BF16)


def grouped(group, bands):
    return bands % group == 0 and bands > group and group & (group - 1) == 0


def gathered(value, group, tie=None, early=None):
    bands = lax.axis_size("band")
    if not grouped(group, bands):
        return [value] + [from_behind(value, "band", a) for a in range(1, group)]
    prior = from_behind(value, "band", group)
    if tie is not None:
        _, prior = lax.optimization_barrier((tie, prior))
    place = lax.axis_index("band") % group
    found = [value]
    sends = [
        jnp.where((place ^ flip) > place, value, prior) for flip in range(1, group)
    ]
    if early is not None:
        sends, early[0] = lax.optimization_barrier((sends, early[0]))
    for flip, sent in enumerate(sends, 1):
        found.append(lax.ppermute(sent, "band", [(b, b ^ flip) for b in range(bands)]))
    return found


def slots_of(order, group):
    offset = order[0]
    if not grouped(group, lax.axis_size("band")):
        return offset
    place = lax.axis_index("band") % group
    return (place ^ ((place - offset + group) % group)).astype(jnp.int32)


def pick(slots_ref, arrays, target):
    count, _, _ = target.shape
    height = arrays[0].shape[0]
    for step in range(count):
        for place, array in enumerate(arrays):
            piece, slot = divmod(place, count)

            @pl.when(slots_ref[step] == slot)
            def _():
                target[step, pl.ds(piece * height, height), :] = array[...]


def cross_kernel(*refs):
    slots_ref, x_ref = refs[:2]
    arrays = refs[2:-2]
    cross_ref, y_ref = refs[-2:]

    @pl.when(pl.program_id(0) == 0)
    def _():
        pick(slots_ref, arrays, y_ref)

    high = x_ref[...].astype(BF16)
    for step in range(y_ref.shape[0]):
        cross_ref[step] = nt(high, y_ref[step])


def block_weight(tables, step, block, cols):
    order_ref, pattern_ref, distance_ref, taper_ref = tables
    q_count = pattern_ref.shape[3]
    width = cols // q_count
    lane = lax.broadcasted_iota(jnp.int32, (1, cols), 1)
    offset = order_ref[0, step]
    weight = jnp.zeros((1, cols), F32)
    for q in range(q_count):
        value = pattern_ref[0, offset, block, q].astype(F32) * taper_ref[
            distance_ref[0, offset, block, q]
        ]
        weight = jnp.where((lane >= q * width) & (lane < (q + 1) * width), value, weight)
    return weight


def link_kernel(*refs):
    slots_ref, y_ref = refs[:2]
    arrays = refs[2:-2]
    g_ref, w_ref = refs[-2:]
    pick(slots_ref, arrays, w_ref)
    place = 0
    for step in range(1, y_ref.shape[0]):
        for before in range(step):
            g_ref[place] = nt(w_ref[before], y_ref[step])
            place += 1


def apply_kernel(scale, per, part_count, *refs):
    tables = refs[:4]
    crosses = refs[4 : 4 + part_count]
    links = refs[4 + part_count : -4]
    w_ref, x_ref, out_ref, link_ref = refs[-4:]
    count, rows, cols = crosses[0].shape

    @pl.when(pl.program_id(0) == 0)
    def _():
        total = links[0][...]
        for part in links[1:]:
            total = total + part[...]
        link_ref[...] = total.astype(BF16)

    applied = []
    field = x_ref[...]
    place = 0
    for step in range(count):
        total = crosses[0][step]
        for part in crosses[1:]:
            total = total + part[step]
        for high in applied:
            total = total + mm(high, link_ref[place])
            place += 1
        weight = jnp.concatenate(
            [
                jnp.broadcast_to(
                    block_weight(tables, step, pl.program_id(0) * per + r, cols), (rows // per, cols)
                )
                for r in range(per)
            ],
            axis=0,
        )
        change = total * scale * weight
        high, low = halves(change)
        applied.append(high)
        field = field + (mm(high, w_ref[step]) + mm(low, w_ref[step]))
    out_ref[...] = field


def on_device(state, obs_anom, innov, pattern, distance, taper, order):
    cells, own_members = state.shape
    members = lax.axis_size("mem") * own_members
    scale = 1.0 / (members - 1)
    num_obs = obs_anom.shape[0]
    arrivals = order.shape[1]
    row_blocks = pattern.shape[2]
    rows = cells // row_blocks
    per = 2 if row_blocks % 2 == 0 else 1
    slots = slots_of(order, arrivals)
    gram_parts = member_parts(nt(obs_anom, obs_anom))
    half = num_obs // 2
    held = [innov]
    ys = gathered(obs_anom[:half], arrivals, early=held)
    innov = held[0]
    solve = pl.pallas_call(
        functools.partial(weigh_kernel, scale, len(gram_parts)),
        out_shape=jax.ShapeDtypeStruct(innov.shape, BF16),
        in_specs=[VMEM_SPEC] * (len(gram_parts) + 1),
        out_specs=VMEM_SPEC,
        scratch_shapes=[pltpu.VMEM((num_obs, num_obs), F32)],
        cost_estimate=pl.CostEstimate(
            flops=60 * num_obs**3, bytes_accessed=8 * innov.size, transcendentals=0
        ),
    )
    weights = solve(*gram_parts, innov)
    slots, weights = lax.optimization_barrier((slots, weights))
    ys = ys + gathered(obs_anom[half:], arrivals, tie=weights)
    ws = gathered(weights, arrivals)
    tall = per * rows
    row_spec = pl.BlockSpec((arrivals, tall, num_obs), lambda i: (0, i, 0))
    field_spec = pl.BlockSpec((tall, own_members), lambda i: (i, 0))
    batch_shape = (arrivals,) + obs_anom.shape
    batch_spec = pl.BlockSpec(batch_shape, lambda i: (0, 0, 0))
    cross_shape = jax.ShapeDtypeStruct((arrivals, cells, num_obs), F32)
    cross_call = pl.pallas_call(
        cross_kernel,
        out_shape=(cross_shape, jax.ShapeDtypeStruct(batch_shape, BF16)),
        grid=(row_blocks // per,),
        in_specs=[SMEM_SPEC, field_spec]
        + [pl.BlockSpec(ys[0].shape, lambda i: (0, 0))] * len(ys),
        out_specs=(row_spec, batch_spec),
        cost_estimate=pl.CostEstimate(
            flops=2 * arrivals * state.size * num_obs, bytes_accessed=12 * state.size, transcendentals=0
        ),
    )
    cross, y_sorted = cross_call(slots, state, *ys)
    crosses = member_parts(cross)
    tables = (order, pattern, distance, taper)
    ws, cross = lax.optimization_barrier((ws, crosses[0]))
    crosses = [cross] + crosses[1:]
    pairs = arrivals * (arrivals - 1) // 2
    link_shape = (pairs, num_obs, num_obs)
    link, w_sorted = pl.pallas_call(
        link_kernel,
        out_shape=(
            jax.ShapeDtypeStruct(link_shape, F32),
            jax.ShapeDtypeStruct(batch_shape, BF16),
        ),
        in_specs=[SMEM_SPEC] + [VMEM_SPEC] * (1 + len(ws)),
        out_specs=(VMEM_SPEC, VMEM_SPEC),
    )(slots, y_sorted, *ws)
    links = member_parts(link)
    return pl.pallas_call(
        functools.partial(apply_kernel, scale, per, len(crosses)),
        out_shape=jax.ShapeDtypeStruct(state.shape, F32),
        grid=(row_blocks // per,),
        in_specs=[SMEM_SPEC] * 4
        + [row_spec] * len(crosses)
        + [pl.BlockSpec(link_shape, lambda i: (0, 0, 0))] * len(links)
        + [batch_spec, field_spec],
        out_specs=field_spec,
        scratch_shapes=[pltpu.VMEM(link_shape, BF16)],
    )(*tables, *crosses, *links, w_sorted, state)


def solution(mesh):
    return jax.shard_map(
        on_device,
        mesh=mesh,
        in_specs=(
            P("band", "mem"),
            P("band", "mem"),
            P("band", "mem"),
            P("band", None, None, None),
            P("band", None, None, None),
            P(),
            P("band", None),
        ),
        out_specs=P("band", "mem"),
        check_vma=False,
    )
```

```python
import functools

import jax
import jax.numpy as jnp
from jax import lax
from jax.experimental import pallas as pl
from jax.experimental.pallas import tpu as pltpu
from jax.sharding import PartitionSpec as P


F32 = jnp.float32
BF16 = jnp.bfloat16
VMEM_SPEC = pl.BlockSpec(memory_space=pltpu.VMEM)
SMEM_SPEC = pl.BlockSpec(memory_space=pltpu.SMEM)


def from_behind(value, axis, steps):
    count = lax.axis_size(axis)
    pairs = [(source, (source + steps) % count) for source in range(count)]
    return lax.ppermute(value, axis, pairs)


def member_parts(value):
    if lax.axis_size("mem") == 2:
        return [value, from_behind(value, "mem", 1)]
    return [lax.psum(value, "mem")]


def halves(value):
    high = value.astype(BF16)
    return high, (value - high.astype(F32)).astype(BF16)


def mm(a, b):
    return jnp.dot(a, b, preferred_element_type=F32)


def mm3(a, b):
    a_high, a_low = halves(a)
    b_high, b_low = halves(b)
    return mm(a_high, b_high) + (mm(a_high, b_low) + mm(a_low, b_high))


def mm_full(a, b):
    return jnp.dot(a, b, precision=lax.Precision.HIGHEST, preferred_element_type=F32)


def nt(a, b):
    return lax.dot_general(a, b, (((1,), (1,)), ((), ())), preferred_element_type=F32)


def weigh_kernel(scale, part_count, *refs):
    parts = refs[:part_count]
    d_ref, w_ref, inv = refs[part_count:]
    total = parts[0][...]
    for part in parts[1:]:
        total = total + part[...]
    size = total.shape[0]
    eye = (
        lax.broadcasted_iota(jnp.int32, (size, size), 0)
        == lax.broadcasted_iota(jnp.int32, (size, size), 1)
    ).astype(F32)
    spd = total * scale + eye
    square = mm3(spd, spd)
    bound2 = jnp.max(jnp.sum(jnp.abs(square), axis=1))
    row = jnp.max(jnp.sum(jnp.abs(spd), axis=1))
    top = jnp.minimum(row, jnp.sqrt(bound2 * 1.01)) * 1.001
    ratio = (top - 1.0) / (top + 1.0)
    alpha = 2.0 / (top + 1.0)
    gain = 2.0 / (2.0 - ratio * ratio)
    c0 = 2.0 * alpha * gain
    c1 = -alpha * alpha * gain
    ratio = ratio * ratio * 0.5 * gain
    inv[...] = c0 * eye + c1 * spd
    small = top < 40.0

    def run(product, active):
        def going(ratio):
            return jnp.logical_and(active, ratio > 2e-5)

        def step(ratio):
            now = inv[...]
            gain = 2.0 / (2.0 - ratio * ratio)
            inv[...] = gain * (2.0 * now - product(now, product(spd, now)))
            return ratio * ratio * 0.5 * gain

        lax.while_loop(going, step, ratio)

    run(mm3, small)
    run(mm_full, jnp.logical_not(small))

    @pl.when(small)
    def _():
        w_ref[...] = mm3(inv[...], d_ref[...]).astype(BF16)

    @pl.when(jnp.logical_not(small))
    def _():
        now = inv[...]
        first = mm_full(now, d_ref[...])
        left = d_ref[...] - mm_full(spd, first)
        w_ref[...] = (first + mm_full(now, left)).astype(BF16)


def grouped(group, bands):
    return bands % group == 0 and bands > group and group & (group - 1) == 0


def gathered(value, group):
    bands = lax.axis_size("band")
    if not grouped(group, bands):
        return [value] + [from_behind(value, "band", a) for a in range(1, group)]
    prior = from_behind(value, "band", group)
    place = lax.axis_index("band") % group
    found = [value]
    sends = [
        jnp.where((place ^ flip) > place, value, prior) for flip in range(1, group)
    ]
    for flip, sent in enumerate(sends, 1):
        found.append(lax.ppermute(sent, "band", [(b, b ^ flip) for b in range(bands)]))
    return found


def slots_of(order, group):
    offset = order[0]
    if not grouped(group, lax.axis_size("band")):
        return offset
    place = lax.axis_index("band") % group
    return (place ^ ((place - offset + group) % group)).astype(jnp.int32)


def pick(slots_ref, arrays, target):
    count, _, _ = target.shape
    height = arrays[0].shape[0]
    for step in range(count):
        for place, array in enumerate(arrays):
            piece, slot = divmod(place, count)

            @pl.when(slots_ref[step] == slot)
            def _():
                target[step, pl.ds(piece * height, height), :] = array[...]


def cross_kernel(*refs):
    slots_ref, x_ref = refs[:2]
    arrays = refs[2:-2]
    cross_ref, y_ref = refs[-2:]

    @pl.when(pl.program_id(0) == 0)
    def _():
        pick(slots_ref, arrays, y_ref)

    high = x_ref[...].astype(BF16)
    for step in range(y_ref.shape[0]):
        cross_ref[step] = nt(high, y_ref[step])


def block_weight(tables, step, block, cols):
    order_ref, pattern_ref, distance_ref, taper_ref = tables
    q_count = pattern_ref.shape[3]
    width = cols // q_count
    lane = lax.broadcasted_iota(jnp.int32, (1, cols), 1)
    offset = order_ref[0, step]
    weight = jnp.zeros((1, cols), F32)
    for q in range(q_count):
        value = pattern_ref[0, offset, block, q].astype(F32) * taper_ref[
            distance_ref[0, offset, block, q]
        ]
        weight = jnp.where((lane >= q * width) & (lane < (q + 1) * width), value, weight)
    return weight


def link_kernel(*refs):
    slots_ref, y_ref = refs[:2]
    arrays = refs[2:-2]
    g_ref, w_ref = refs[-2:]
    pick(slots_ref, arrays, w_ref)
    place = 0
    for step in range(1, y_ref.shape[0]):
        for before in range(step):
            g_ref[place] = nt(w_ref[before], y_ref[step])
            place += 1


def apply_kernel(scale, per, part_count, *refs):
    tables = refs[:4]
    crosses = refs[4 : 4 + part_count]
    links = refs[4 + part_count : -4]
    w_ref, x_ref, out_ref, link_ref = refs[-4:]
    count, rows, cols = crosses[0].shape

    @pl.when(pl.program_id(0) == 0)
    def _():
        total = links[0][...]
        for part in links[1:]:
            total = total + part[...]
        link_ref[...] = total.astype(BF16)

    applied = []
    field = x_ref[...]
    place = 0
    for step in range(count):
        total = crosses[0][step]
        for part in crosses[1:]:
            total = total + part[step]
        for high in applied:
            total = total + mm(high, link_ref[place])
            place += 1
        weight = jnp.concatenate(
            [
                jnp.broadcast_to(
                    block_weight(tables, step, pl.program_id(0) * per + r, cols), (rows // per, cols)
                )
                for r in range(per)
            ],
            axis=0,
        )
        change = total * scale * weight
        high, low = halves(change)
        applied.append(high)
        field = field + (mm(high, w_ref[step]) + mm(low, w_ref[step]))
    out_ref[...] = field


def on_device(state, obs_anom, innov, pattern, distance, taper, order):
    cells, own_members = state.shape
    members = lax.axis_size("mem") * own_members
    scale = 1.0 / (members - 1)
    num_obs = obs_anom.shape[0]
    arrivals = order.shape[1]
    row_blocks = pattern.shape[2]
    rows = cells // row_blocks
    per = 2 if row_blocks % 2 == 0 else 1
    slots = slots_of(order, arrivals)
    gram_parts = member_parts(nt(obs_anom, obs_anom))
    ys = gathered(obs_anom, arrivals)
    solve = pl.pallas_call(
        functools.partial(weigh_kernel, scale, len(gram_parts)),
        out_shape=jax.ShapeDtypeStruct(innov.shape, BF16),
        in_specs=[VMEM_SPEC] * (len(gram_parts) + 1),
        out_specs=VMEM_SPEC,
        scratch_shapes=[pltpu.VMEM((num_obs, num_obs), F32)],
        cost_estimate=pl.CostEstimate(
            flops=60 * num_obs**3, bytes_accessed=8 * innov.size, transcendentals=0
        ),
    )
    weights = solve(*gram_parts, innov)
    slots, weights = lax.optimization_barrier((slots, weights))
    ws = gathered(weights, arrivals)
    tall = per * rows
    row_spec = pl.BlockSpec((arrivals, tall, num_obs), lambda i: (0, i, 0))
    field_spec = pl.BlockSpec((tall, own_members), lambda i: (i, 0))
    batch_shape = (arrivals,) + obs_anom.shape
    batch_spec = pl.BlockSpec(batch_shape, lambda i: (0, 0, 0))
    cross_shape = jax.ShapeDtypeStruct((arrivals, cells, num_obs), F32)
    cross_call = pl.pallas_call(
        cross_kernel,
        out_shape=(cross_shape, jax.ShapeDtypeStruct(batch_shape, BF16)),
        grid=(row_blocks // per,),
        in_specs=[SMEM_SPEC, field_spec]
        + [pl.BlockSpec(ys[0].shape, lambda i: (0, 0))] * len(ys),
        out_specs=(row_spec, batch_spec),
        cost_estimate=pl.CostEstimate(
            flops=2 * arrivals * state.size * num_obs, bytes_accessed=12 * state.size, transcendentals=0
        ),
    )
    cross, y_sorted = cross_call(slots, state, *ys)
    crosses = member_parts(cross)
    tables = (order, pattern, distance, taper)
    ws, cross = lax.optimization_barrier((ws, crosses[0]))
    crosses = [cross] + crosses[1:]
    pairs = arrivals * (arrivals - 1) // 2
    link_shape = (pairs, num_obs, num_obs)
    link, w_sorted = pl.pallas_call(
        link_kernel,
        out_shape=(
            jax.ShapeDtypeStruct(link_shape, F32),
            jax.ShapeDtypeStruct(batch_shape, BF16),
        ),
        in_specs=[SMEM_SPEC] + [VMEM_SPEC] * (1 + len(ws)),
        out_specs=(VMEM_SPEC, VMEM_SPEC),
    )(slots, y_sorted, *ws)
    links = member_parts(link)
    return pl.pallas_call(
        functools.partial(apply_kernel, scale, per, len(crosses)),
        out_shape=jax.ShapeDtypeStruct(state.shape, F32),
        grid=(row_blocks // per,),
        in_specs=[SMEM_SPEC] * 4
        + [row_spec] * len(crosses)
        + [pl.BlockSpec(link_shape, lambda i: (0, 0, 0))] * len(links)
        + [batch_spec, field_spec],
        out_specs=field_spec,
        scratch_shapes=[pltpu.VMEM(link_shape, BF16)],
    )(*tables, *crosses, *links, w_sorted, state)


def solution(mesh):
    return jax.shard_map(
        on_device,
        mesh=mesh,
        in_specs=(
            P("band", "mem"),
            P("band", "mem"),
            P("band", "mem"),
            P("band", None, None, None),
            P("band", None, None, None),
            P(),
            P("band", None),
        ),
        out_specs=P("band", "mem"),
        check_vma=False,
    )
```

```python
import functools

import jax
import jax.numpy as jnp
from jax import lax
from jax.experimental import pallas as pl
from jax.experimental.pallas import tpu as pltpu
from jax.sharding import PartitionSpec as P


F32 = jnp.float32
BF16 = jnp.bfloat16
VMEM_SPEC = pl.BlockSpec(memory_space=pltpu.VMEM)
SMEM_SPEC = pl.BlockSpec(memory_space=pltpu.SMEM)


def from_behind(value, axis, steps):
    count = lax.axis_size(axis)
    pairs = [(source, (source + steps) % count) for source in range(count)]
    return lax.ppermute(value, axis, pairs)


def member_parts(value):
    if lax.axis_size("mem") == 2:
        return [value, from_behind(value, "mem", 1)]
    return [lax.psum(value, "mem")]


def halves(value):
    high = value.astype(BF16)
    return high, (value - high.astype(F32)).astype(BF16)


def mm(a, b):
    return jnp.dot(a, b, preferred_element_type=F32)


def mm3(a, b):
    a_high, a_low = halves(a)
    b_high, b_low = halves(b)
    return mm(a_high, b_high) + (mm(a_high, b_low) + mm(a_low, b_high))


def mm_full(a, b):
    return jnp.dot(a, b, precision=lax.Precision.HIGHEST, preferred_element_type=F32)


def nt(a, b):
    return lax.dot_general(a, b, (((1,), (1,)), ((), ())), preferred_element_type=F32)


def weigh_kernel(scale, part_count, *refs):
    parts = refs[:part_count]
    d_ref, w_ref, inv = refs[part_count:]
    total = parts[0][...]
    for part in parts[1:]:
        total = total + part[...]
    size = total.shape[0]
    eye = (
        lax.broadcasted_iota(jnp.int32, (size, size), 0)
        == lax.broadcasted_iota(jnp.int32, (size, size), 1)
    ).astype(F32)
    spd = total * scale + eye
    square = mm3(spd, spd)
    bound2 = jnp.max(jnp.sum(jnp.abs(square), axis=1))
    row = jnp.max(jnp.sum(jnp.abs(spd), axis=1))
    top = jnp.minimum(row, jnp.sqrt(bound2 * 1.01)) * 1.001
    ratio = (top - 1.0) / (top + 1.0)
    alpha = 2.0 / (top + 1.0)
    gain = 2.0 / (2.0 - ratio * ratio)
    c0 = 2.0 * alpha * gain
    c1 = -alpha * alpha * gain
    ratio = ratio * ratio * 0.5 * gain
    inv[...] = c0 * eye + c1 * spd
    small = top < 40.0

    def run(product, active):
        def going(ratio):
            return jnp.logical_and(active, ratio > 2e-5)

        def step(ratio):
            now = inv[...]
            gain = 2.0 / (2.0 - ratio * ratio)
            inv[...] = gain * (2.0 * now - product(now, product(spd, now)))
            return ratio * ratio * 0.5 * gain

        lax.while_loop(going, step, ratio)

    run(mm3, small)
    run(mm_full, jnp.logical_not(small))

    @pl.when(small)
    def _():
        w_ref[...] = mm3(inv[...], d_ref[...]).astype(BF16)

    @pl.when(jnp.logical_not(small))
    def _():
        now = inv[...]
        first = mm_full(now, d_ref[...])
        left = d_ref[...] - mm_full(spd, first)
        w_ref[...] = (first + mm_full(now, left)).astype(BF16)


def grouped(group, bands):
    return bands % group == 0 and bands > group and group & (group - 1) == 0


def gathered(value, group):
    bands = lax.axis_size("band")
    if not grouped(group, bands):
        return [value] + [from_behind(value, "band", a) for a in range(1, group)]
    prior = from_behind(value, "band", group)
    place = lax.axis_index("band") % group
    found = [value]
    sends = [
        jnp.where((place ^ flip) > place, value, prior) for flip in range(1, group)
    ]
    for flip, sent in enumerate(sends, 1):
        found.append(lax.ppermute(sent, "band", [(b, b ^ flip) for b in range(bands)]))
    return found


def slots_of(order, group):
    offset = order[0]
    if not grouped(group, lax.axis_size("band")):
        return offset
    place = lax.axis_index("band") % group
    return (place ^ ((place - offset + group) % group)).astype(jnp.int32)


def pick(slots_ref, arrays, target):
    count, _, _ = target.shape
    height = arrays[0].shape[0]
    for step in range(count):
        for place, array in enumerate(arrays):
            piece, slot = divmod(place, count)

            @pl.when(slots_ref[step] == slot)
            def _():
                target[step, pl.ds(piece * height, height), :] = array[...]


def cross_kernel(*refs):
    slots_ref, x_ref = refs[:2]
    arrays = refs[2:-2]
    cross_ref, y_ref = refs[-2:]

    @pl.when(pl.program_id(0) == 0)
    def _():
        pick(slots_ref, arrays, y_ref)

    high = x_ref[...].astype(BF16)
    for step in range(y_ref.shape[0]):
        cross_ref[step] = nt(high, y_ref[step])


def block_weight(tables, step, block, cols):
    order_ref, pattern_ref, distance_ref, taper_ref = tables
    q_count = pattern_ref.shape[3]
    width = cols // q_count
    lane = lax.broadcasted_iota(jnp.int32, (1, cols), 1)
    offset = order_ref[0, step]
    weight = jnp.zeros((1, cols), F32)
    for q in range(q_count):
        value = pattern_ref[0, offset, block, q].astype(F32) * taper_ref[
            distance_ref[0, offset, block, q]
        ]
        weight = jnp.where((lane >= q * width) & (lane < (q + 1) * width), value, weight)
    return weight


def link_kernel(*refs):
    slots_ref, y_ref = refs[:2]
    arrays = refs[2:-2]
    g_ref, w_ref = refs[-2:]
    pick(slots_ref, arrays, w_ref)
    place = 0
    for step in range(1, y_ref.shape[0]):
        for before in range(step):
            g_ref[place] = nt(w_ref[before], y_ref[step]).astype(BF16)
            place += 1


def apply_kernel(scale, per, part_count, *refs):
    tables = refs[:4]
    crosses = refs[4 : 4 + part_count]
    links = refs[4 + part_count : -4]
    w_ref, x_ref, out_ref, link_ref = refs[-4:]
    count, rows, cols = crosses[0].shape

    @pl.when(pl.program_id(0) == 0)
    def _():
        total = links[0][...].astype(F32)
        for part in links[1:]:
            total = total + part[...].astype(F32)
        link_ref[...] = total.astype(BF16)

    applied = []
    field = x_ref[...]
    place = 0
    for step in range(count):
        total = crosses[0][step]
        for part in crosses[1:]:
            total = total + part[step]
        for high in applied:
            total = total + mm(high, link_ref[place])
            place += 1
        weight = jnp.concatenate(
            [
                jnp.broadcast_to(
                    block_weight(tables, step, pl.program_id(0) * per + r, cols), (rows // per, cols)
                )
                for r in range(per)
            ],
            axis=0,
        )
        change = total * scale * weight
        high, low = halves(change)
        applied.append(high)
        field = field + (mm(high, w_ref[step]) + mm(low, w_ref[step]))
    out_ref[...] = field


def on_device(state, obs_anom, innov, pattern, distance, taper, order):
    cells, own_members = state.shape
    members = lax.axis_size("mem") * own_members
    scale = 1.0 / (members - 1)
    num_obs = obs_anom.shape[0]
    arrivals = order.shape[1]
    row_blocks = pattern.shape[2]
    rows = cells // row_blocks
    per = 2 if row_blocks % 2 == 0 else 1
    slots = slots_of(order, arrivals)
    gram_parts = member_parts(nt(obs_anom, obs_anom))
    ys = gathered(obs_anom, arrivals)
    solve = pl.pallas_call(
        functools.partial(weigh_kernel, scale, len(gram_parts)),
        out_shape=jax.ShapeDtypeStruct(innov.shape, BF16),
        in_specs=[VMEM_SPEC] * (len(gram_parts) + 1),
        out_specs=VMEM_SPEC,
        scratch_shapes=[pltpu.VMEM((num_obs, num_obs), F32)],
        cost_estimate=pl.CostEstimate(
            flops=60 * num_obs**3, bytes_accessed=8 * innov.size, transcendentals=0
        ),
    )
    weights = solve(*gram_parts, innov)
    slots, weights = lax.optimization_barrier((slots, weights))
    ws = gathered(weights, arrivals)
    tall = per * rows
    row_spec = pl.BlockSpec((arrivals, tall, num_obs), lambda i: (0, i, 0))
    field_spec = pl.BlockSpec((tall, own_members), lambda i: (i, 0))
    batch_shape = (arrivals,) + obs_anom.shape
    batch_spec = pl.BlockSpec(batch_shape, lambda i: (0, 0, 0))
    cross_shape = jax.ShapeDtypeStruct((arrivals, cells, num_obs), F32)
    cross_call = pl.pallas_call(
        cross_kernel,
        out_shape=(cross_shape, jax.ShapeDtypeStruct(batch_shape, BF16)),
        grid=(row_blocks // per,),
        in_specs=[SMEM_SPEC, field_spec]
        + [pl.BlockSpec(ys[0].shape, lambda i: (0, 0))] * len(ys),
        out_specs=(row_spec, batch_spec),
        cost_estimate=pl.CostEstimate(
            flops=2 * arrivals * state.size * num_obs, bytes_accessed=12 * state.size, transcendentals=0
        ),
    )
    cross, y_sorted = cross_call(slots, state, *ys)
    crosses = member_parts(cross)
    tables = (order, pattern, distance, taper)
    ws, cross = lax.optimization_barrier((ws, crosses[0]))
    crosses = [cross] + crosses[1:]
    pairs = arrivals * (arrivals - 1) // 2
    link_shape = (pairs, num_obs, num_obs)
    link, w_sorted = pl.pallas_call(
        link_kernel,
        out_shape=(
            jax.ShapeDtypeStruct(link_shape, BF16),
            jax.ShapeDtypeStruct(batch_shape, BF16),
        ),
        in_specs=[SMEM_SPEC] + [VMEM_SPEC] * (1 + len(ws)),
        out_specs=(VMEM_SPEC, VMEM_SPEC),
    )(slots, y_sorted, *ws)
    links = member_parts(link)
    return pl.pallas_call(
        functools.partial(apply_kernel, scale, per, len(crosses)),
        out_shape=jax.ShapeDtypeStruct(state.shape, F32),
        grid=(row_blocks // per,),
        in_specs=[SMEM_SPEC] * 4
        + [row_spec] * len(crosses)
        + [pl.BlockSpec(link_shape, lambda i: (0, 0, 0))] * len(links)
        + [batch_spec, field_spec],
        out_specs=field_spec,
        scratch_shapes=[pltpu.VMEM(link_shape, BF16)],
    )(*tables, *crosses, *links, w_sorted, state)


def solution(mesh):
    return jax.shard_map(
        on_device,
        mesh=mesh,
        in_specs=(
            P("band", "mem"),
            P("band", "mem"),
            P("band", "mem"),
            P("band", None, None, None),
            P("band", None, None, None),
            P(),
            P("band", None),
        ),
        out_specs=P("band", "mem"),
        check_vma=False,
    )
```
